32 devices in a mesh: snp: 8 (over z, x), trait: 4 (over y, core).
Axes of the slice: x: 2, y: 2, z: 4, core: 2. Of those that a mesh axis runs over, the one named last changes fastest.
Arguments:
- genotype: bfloat16 [32, 8192], P(None, 'snp'), may hold values from -0.0625 to 0.0625
- targets: bfloat16 [32, 16384], P('snp', 'trait'), may hold values from -6 to 6
- effect_sizes: float32 [8192, 16384], P('snp', 'trait'), may hold values from -6 to 6
- membership: int32 [4, 128, 128], replicated, may hold values from 0 to 1, as said below
- node_weight: float32 [4, 128], replicated, may hold values from 0.03 to 1
Outputs:
- updated: float32 [8192, 16384], P('snp', 'trait')
The draws below stay inside these ranges and needn't reach their ends.
Inputs may be any that keep to these rules, and one draw needn't show every extreme that they name: `membership`: at each level the node slots 0 .. c - 1 partition all 128 trait blocks, the remaining slots cover none; every node of a level lies inside one node of the next level; at level 0 each block is its own node.
All inputs are finite; a program needn't handle non-finite values.
Results may differ from the reference program's by a relative error of at most 0.00042.
Values may be sent and summed in bfloat16 or wider, within the bound.
A program may use at most 128 MiB of HBM per device.

```python
import math
import jax
import jax.numpy as jnp
from jax import lax

J = 8192
TB = 128
BLOCKS = 128
LEVELS = 4
ITERS = 1
K = 16384
NODES = 128
N = 32


def draw_membership(key, part):
    order = jax.random.permutation(jax.random.fold_in(key, 1), BLOCKS)
    boundary = jnp.ones((BLOCKS,), jnp.int32)
    first = (jnp.arange(BLOCKS) == 0).astype(jnp.int32)
    slots = jnp.arange(BLOCKS, dtype=jnp.int32)
    levels_out = []
    for level in range(LEVELS):
        if level > 0:
            coin = jax.random.randint(jax.random.fold_in(key, 10 + level), (BLOCKS,), 0, 2)
            boundary = jnp.maximum(boundary * (coin == 0).astype(jnp.int32), first)
        node_pos = (jnp.cumsum(boundary) - 1).astype(jnp.int32)
        node_block = jnp.zeros((BLOCKS,), jnp.int32).at[order].set(node_pos)
        levels_out.append((slots[:, None] == node_block[None, :]).astype(jnp.int32))
    return jnp.stack(levels_out, axis=0)


def level_of(key, dims, cuts, smallest, largest):
    gain, own = 1.0, jax.random.fold_in(key, 6)
    for position, blocks in cuts:
        draws = jnp.exp(jax.random.uniform(jax.random.fold_in(own, position), (blocks,), jnp.float32, smallest / len(cuts), largest / len(cuts)))
        gain = gain * jnp.repeat(draws, dims[position] // blocks).reshape([-1 if axis == position else 1 for axis in range(len(dims))])
    return gain


def gaussian(stream_key, shape, width, most, shards=(), kind=jnp.bfloat16):
    loudness = level_of(stream_key, shape, shards, -0.22, 0.18) if shards else 1.0
    entries = jax.random.normal(stream_key, shape, jnp.float32) * width * loudness
    return jnp.minimum(jnp.maximum(entries, -most), most).astype(kind)


def setup_inputs(seed: int = 0) -> dict:
    key_list = jax.random.split(jax.random.key(seed), 6)
    return {
        "genotype": gaussian(key_list[0], (N, J), J ** -0.5, 0.0625, ((1, 8),)),
        "targets": gaussian(key_list[1], (N, K), 1.0, 6.0, ((0, 8), (1, 4))),
        "effect_sizes": gaussian(key_list[2], (J, K), 1.0, 6.0, ((0, 8), (1, 4)), jnp.float32),
        "membership": draw_membership(jax.random.fold_in(key_list[5], 71), 0),
        "node_weight": jnp.clip(jnp.exp(jax.random.uniform(key_list[4], (LEVELS, NODES), jnp.float32, math.log(0.03), math.log(1.0))), 0.03, 1.0),
    }


step_size = 0.5

def shrink_tree(value, membership, node_weight):
    for level in range(LEVELS):
        member = membership[level].astype(jnp.float32)
        count = lax.optimization_barrier(jnp.sum(member, axis=1))
        threshold = step_size * node_weight[level] * jnp.sqrt(TB * jnp.maximum(count, 1.0))
        blocks = value.reshape(value.shape[0], BLOCKS, TB)
        block_sq = lax.optimization_barrier(jnp.sum(blocks * blocks, axis=2))
        node_sq = jnp.dot(block_sq, member.T, precision=lax.Precision.HIGHEST)
        norm = jnp.sqrt(node_sq)
        factor = jnp.maximum(norm - threshold, 0.0) / jnp.maximum(norm, threshold)
        block_factor = jnp.dot(factor, member, precision=lax.Precision.HIGHEST)
        value = (blocks * block_factor[:, :, None]).reshape(value.shape)
    return value

def reference(genotype, targets, effect_sizes, membership, node_weight):
    current = effect_sizes
    for sweep_index in range(ITERS):
        current_bf = current.astype(jnp.bfloat16)
        fitted = jnp.dot(genotype, current_bf, preferred_element_type=jnp.float32)
        residual = (targets.astype(jnp.float32) - fitted).astype(jnp.bfloat16)
        gradient = lax.dot_general(genotype, residual, (((0,), (0,)), ((), ())), preferred_element_type=jnp.float32)
        current = shrink_tree(current + step_size * gradient, membership, node_weight)
    return current
```

```python
import functools

import jax
import jax.numpy as jnp
from jax import lax
from jax.experimental import pallas as pl
from jax.experimental.pallas import tpu as pltpu
from jax.sharding import PartitionSpec as P

TB = 128
SUB = 16
STEP = 0.5
F32 = jnp.float32
BF16 = jnp.bfloat16
MESH = pl.DeviceIdType.MESH
HIGH = lax.Precision.HIGHEST
TN = (((0,), (0,)), ((), ()))
TT = (((0,), (1,)), ((), ()))


def one_hot_rows(slots, samples, per, group, owner_of, gain):
    r = lax.broadcasted_iota(jnp.int32, (slots * SUB, samples), 0)
    n = lax.broadcasted_iota(jnp.int32, (slots * SUB, samples), 1)
    owner = owner_of(lax.shift_right_logical(r, 4))
    inner = jnp.bitwise_and(r, SUB - 1) - group * per
    hit = (n == owner * per + inner) & (inner >= 0) & (inner < per)
    return jnp.where(hit, gain, 0.0).astype(BF16)


def split3(x):
    hi = x.astype(BF16)
    x = x - hi.astype(F32)
    mid = x.astype(BF16)
    low = (x - mid.astype(F32)).astype(BF16)
    return jnp.concatenate([hi, mid, low], axis=0)


def fit_kernel(
    n, trait, widths, row_tile,
    g_ref, t_ref, m_ref, w_ref, e_hbm,
    v_ref, sc_ref,
    send, got, rg, tq, gs, gt, gq, ssum, thr,
    e_sem, rs_send, rs_recv, ag_send, ag_recv, x_send, x_recv,
):
    me = lax.axis_index("snp")
    mt = lax.axis_index("trait")
    samples, rows = g_ref.shape
    per = samples // n
    groups = SUB // per
    cols = v_ref.shape[1]
    blocks = cols // TB
    levels = m_ref.shape[0]
    chunks = len(widths)
    first = [sum(widths[:c]) for c in range(chunks)]

    def part(c):
        return pl.ds(first[c], widths[c])

    def cols_of(c, h):
        return pl.ds(groups * first[c] + h * widths[c], widths[c])

    def chunk_blocks(c):
        return pl.ds(groups * first[c] // TB, groups * widths[c] // TB)

    def load(c):
        span = pl.ds(groups * first[c], groups * widths[c])
        return pltpu.make_async_copy(e_hbm.at[:, span], v_ref.at[:, span], e_sem.at[c])

    for c in range(chunks):
        load(c).start()

    def peers(count, fn):
        if count <= 8:
            for k in range(count - 1, 0, -1):
                fn(k)
        else:
            lax.fori_loop(1, count, lambda k, _: (fn(k), 0)[1], 0)

    barrier = pltpu.get_barrier_semaphore()

    def greet(axis, own):
        def one(k):
            pl.semaphore_signal(
                barrier, inc=1, device_id={axis: jnp.bitwise_xor(own, k)}, device_id_type=MESH
            )
        return one

    peers(n, greet("snp", me))
    peers(trait, greet("trait", mt))

    def rs_copy(c, k):
        to = jnp.bitwise_xor(me, k)
        return pltpu.make_async_remote_copy(
            src_ref=send.at[to, :, part(c)],
            dst_ref=got.at[k, :, part(c)],
            send_sem=rs_send,
            recv_sem=rs_recv.at[c],
            device_id={"snp": to},
            device_id_type=MESH,
        )

    def ag_copy(c, k):
        return pltpu.make_async_remote_copy(
            src_ref=rg.at[0, :, part(c)],
            dst_ref=rg.at[k, :, part(c)],
            send_sem=ag_send,
            recv_sem=ag_recv.at[c],
            device_id={"snp": jnp.bitwise_xor(me, k)},
            device_id_type=MESH,
        )

    def x_copy(c, k):
        return pltpu.make_async_remote_copy(
            src_ref=gq.at[0, chunk_blocks(c), :],
            dst_ref=gq.at[k, chunk_blocks(c), :],
            send_sem=x_send,
            recv_sem=x_recv,
            device_id={"trait": jnp.bitwise_xor(mt, k)},
            device_id_type=MESH,
        )

    def drain(ref, sem):
        pltpu.make_async_copy(ref, ref, sem).wait()

    for h in range(groups):
        pick = one_hot_rows(n, samples, per, h, lambda s: s, 1.0)
        gs[h] = jnp.dot(pick, g_ref[...], preferred_element_type=F32).astype(BF16)
    for c in range(chunks):
        tq[:, part(c)] = jnp.concatenate(
            [t_ref[:, cols_of(c, h)].astype(F32) for h in range(groups)], axis=0
        )

    def prepare_rows():
        for h in range(groups):
            pick = one_hot_rows(
                n, samples, per, h, lambda s: jnp.bitwise_xor(s, me), STEP
            )
            gt[h] = lax.dot_general(
                g_ref[...], pick, TT, preferred_element_type=F32
            ).astype(BF16)

    def prepare_level(level):
        shape = (trait * blocks, trait * blocks)
        a = lax.broadcasted_iota(jnp.int32, shape, 0)
        r = lax.broadcasted_iota(jnp.int32, shape, 1)
        slot = r // blocks
        there = jnp.bitwise_xor(slot, mt) * blocks + (r - slot * blocks)
        order = jnp.where(a == there, 1.0, 0.0).astype(BF16)
        member = m_ref[level].astype(F32)
        count = jnp.sum(member, axis=1, keepdims=True)
        member = jnp.dot(member.astype(BF16), order, preferred_element_type=F32)
        weight = jnp.broadcast_to(w_ref[level : level + 1, :], (TB, member.shape[0])).T
        by_node = STEP * weight * jnp.sqrt(TB * jnp.maximum(count, 1.0))
        thr[level] = lax.dot_general(
            member, by_node, TN, precision=HIGH, preferred_element_type=F32
        )
        near = member.astype(BF16)
        ssum[level] = lax.dot_general(near, near, TN, preferred_element_type=F32).astype(BF16)

    kt = min(rows, 256)

    def fit_chunk(c):
        load(c).wait()
        total = jnp.zeros((n * SUB, widths[c]), F32)
        for h in range(groups):
            for k in range(rows // kt):
                total += jnp.dot(
                    gs[h, :, k * kt : (k + 1) * kt],
                    v_ref[k * kt : (k + 1) * kt, cols_of(c, h)].astype(BF16),
                    preferred_element_type=F32,
                )
        send[:, :, part(c)] = total.astype(BF16).reshape(n, SUB, widths[c])
        if c == 0:
            pl.semaphore_wait(barrier, n + trait - 2)
        peers(n, lambda k: rs_copy(c, k).start())

    def res_chunk(c):
        drain(got.at[pl.ds(1, n - 1), :, part(c)], rs_recv.at[c])
        fitted = send[me, :, part(c)].astype(F32)
        fitted += jnp.sum(got[1:, :, part(c)].astype(F32), axis=0)
        rg[0, :, part(c)] = (tq[:, part(c)] - fitted).astype(BF16)
        peers(n, lambda k: ag_copy(c, k).start())

    def value_chunk(c):
        w = widths[c]
        drain(rg.at[pl.ds(1, n - 1), :, part(c)], ag_recv.at[c])
        resid = rg[:, :, part(c)].reshape(n * SUB, w)
        lane = lax.broadcasted_iota(jnp.int32, (row_tile, TB), 1)
        many = groups * w // TB
        for i in range(rows // row_tile):
            r = pl.ds(i * row_tile, row_tile)
            sums = jnp.zeros((row_tile, TB), F32)
            for h in range(groups):
                grad = jnp.dot(gt[h, r, :], resid, preferred_element_type=F32)
                value = v_ref[r, cols_of(c, h)] + grad
                v_ref[r, cols_of(c, h)] = value
                sq = value * value
                for b in range(w // TB):
                    s = jnp.sum(sq[:, b * TB : (b + 1) * TB], axis=1, keepdims=True)
                    sums = jnp.where(lane == h * (w // TB) + b, s, sums)
            gq[0, chunk_blocks(c), r] = sums.T[:many]
        peers(trait, lambda k: x_copy(c, k).start())

    for c in range(chunks):
        fit_chunk(c)
        if c == 0:
            prepare_level(0)
            prepare_level(1)
        elif c == 1:
            prepare_level(2)
            prepare_level(3)
        elif c == 2:
            prepare_rows()
    for c in range(chunks):
        res_chunk(c)
    for c in range(chunks):
        value_chunk(c)

    drain(send.at[pl.ds(1, n - 1)], rs_send)
    drain(rg.at[pl.ds(1, n - 1)], ag_send)
    drain(gq.at[pl.ds(1, trait - 1)], x_recv)

    block_sq = gq[...].reshape(trait * blocks, rows)
    scale = None
    for level in range(levels):
        if level == 0:
            node_sq = block_sq
        else:
            node_sq = jnp.dot(
                jnp.concatenate([ssum[level]] * 3, axis=1),
                split3(block_sq),
                preferred_element_type=F32,
            )
        factor = jnp.maximum(1.0 - thr[level][:, :1] * lax.rsqrt(node_sq), 0.0)
        scale = factor[:blocks] if scale is None else scale * factor[:blocks]
        block_sq = block_sq * (factor * factor)
    sc_ref[:, :blocks] = scale.T
    drain(gq.at[pl.ds(1, trait - 1)], x_send)


def scale_kernel(pieces, row_tile, v_ref, sc_ref, o_hbm, out, sem):
    rows, cols = v_ref.shape
    size = rows // pieces

    def store(p):
        r = pl.ds(pl.multiple_of(p * size, size), size)
        return pltpu.make_async_copy(out.at[r, :], o_hbm.at[r, :], sem.at[p])

    def piece(p, _):
        def tile(i, _):
            start = pl.multiple_of(p * size + i * row_tile, row_tile)
            r = pl.ds(start, row_tile)
            sc = sc_ref[r, :]
            for b in range(cols // TB):
                c = slice(b * TB, (b + 1) * TB)
                out[r, c] = v_ref[r, c] * sc[:, b : b + 1]
            return 0

        lax.fori_loop(0, size // row_tile, tile, 0)
        store(p).start()
        return 0

    lax.fori_loop(0, pieces, piece, 0)
    lax.fori_loop(0, pieces, lambda p, _: (store(p).wait(), 0)[1], 0)


def body(n, trait, genotype, targets, effect_sizes, membership, node_weight):
    samples, rows = genotype.shape
    cols = effect_sizes.shape[1]
    blocks = cols // TB
    levels = membership.shape[0]
    groups = SUB // (samples // n)
    lines = cols // groups
    chunks = 4
    widths = [lines // chunks] * chunks
    vmem = pl.BlockSpec(memory_space=pltpu.VMEM)
    hbm = pl.BlockSpec(memory_space=pl.ANY)
    dma = pltpu.SemaphoreType.DMA
    value, scale = pl.pallas_call(
        functools.partial(fit_kernel, n, trait, widths, rows),
        name="fit",
        out_shape=(pltpu.VMEM((rows, cols), F32), pltpu.VMEM((rows, TB), F32)),
        in_specs=[vmem] * 4 + [hbm],
        out_specs=(vmem, vmem),
        scratch_shapes=[
            pltpu.VMEM((n, SUB, lines), BF16),
            pltpu.VMEM((n, SUB, lines), BF16),
            pltpu.VMEM((n, SUB, lines), BF16),
            pltpu.VMEM((SUB, lines), F32),
            pltpu.VMEM((groups, n * SUB, rows), BF16),
            pltpu.VMEM((groups, rows, n * SUB), BF16),
            pltpu.VMEM((trait, blocks, rows), F32),
            pltpu.VMEM((levels, trait * blocks, trait * blocks), BF16),
            pltpu.VMEM((levels, trait * blocks, TB), F32),
            dma((chunks,)),
            dma,
            dma((chunks,)),
            dma,
            dma((chunks,)),
            dma,
            dma,
        ],
        compiler_params=pltpu.CompilerParams(
            collective_id=0, has_side_effects=True, vmem_limit_bytes=40 << 20
        ),
    )(genotype, targets, membership, node_weight, effect_sizes)
    value = pltpu.with_memory_space_constraint(value, pltpu.VMEM)
    scale = pltpu.with_memory_space_constraint(scale, pltpu.VMEM)
    pieces = 8
    return pl.pallas_call(
        functools.partial(scale_kernel, pieces, min(rows // pieces, 128)),
        name="scale",
        out_shape=jax.ShapeDtypeStruct((rows, cols), F32),
        in_specs=[vmem, vmem],
        out_specs=hbm,
        scratch_shapes=[pltpu.VMEM((rows, cols), F32), dma((pieces,))],
        compiler_params=pltpu.CompilerParams(vmem_limit_bytes=40 << 20),
    )(value, scale)


def solution(mesh):
    n, trait = mesh.shape["snp"], mesh.shape["trait"]
    return jax.shard_map(
        functools.partial(body, n, trait),
        mesh=mesh,
        in_specs=(P(None, "snp"), P("snp", "trait"), P("snp", "trait"), P(), P()),
        out_specs=P("snp", "trait"),
        check_vma=False,
    )
```

```python
import functools

import jax
import jax.numpy as jnp
from jax import lax
from jax.experimental import pallas as pl
from jax.experimental.pallas import tpu as pltpu
from jax.sharding import PartitionSpec as P

TB = 128
SUB = 16
STEP = 0.5
F32 = jnp.float32
BF16 = jnp.bfloat16
MESH = pl.DeviceIdType.MESH
TN = (((0,), (0,)), ((), ()))
TT = (((0,), (1,)), ((), ()))


def one_hot_rows(slots, samples, per, group, gain):
    r = lax.broadcasted_iota(jnp.int32, (slots * SUB, samples), 0)
    n = lax.broadcasted_iota(jnp.int32, (slots * SUB, samples), 1)
    owner = lax.shift_right_logical(r, 4)
    inner = jnp.bitwise_and(r, SUB - 1) - group * per
    hit = (n == owner * per + inner) & (inner >= 0) & (inner < per)
    return jnp.where(hit, gain, 0.0).astype(BF16)


def split3(x):
    hi = x.astype(BF16)
    x = x - hi.astype(F32)
    mid = x.astype(BF16)
    low = (x - mid.astype(F32)).astype(BF16)
    return jnp.concatenate([hi, mid, low], axis=0)


def fit_kernel(
    n, trait, widths, plan,
    g_hbm, t_hbm, m_hbm, w_hbm, e_hbm,
    v_ref, sc_ref, *scratch,
):
    chunks = len(widths)
    send, got, rg, gq = (scratch[i * chunks : (i + 1) * chunks] for i in range(4))
    g_ref, t_ref, m_ref, w_ref, ts, gs, gt, ssum, thr, s_sem, e_sem, out_sem, in_sem = scratch[4 * chunks :]
    me = lax.axis_index("snp")
    mt = lax.axis_index("trait")
    samples, rows = g_ref.shape
    owners = n // 2
    base = n // 4
    per = samples // owners
    groups = SUB // per
    mine = me - base
    is_owner = (mine >= 0) & (mine < owners)
    cols = v_ref.shape[1]
    blocks = cols // TB
    levels = m_ref.shape[0]
    first = [sum(widths[:c]) for c in range(chunks)]

    def snp_peer(slot):
        return {"snp": jnp.bitwise_xor(me, slot)}

    def cols_of(c, h):
        return pl.ds(groups * first[c] + h * widths[c], widths[c])

    def load(c):
        span = pl.ds(groups * first[c], groups * widths[c])
        return pltpu.make_async_copy(e_hbm.at[:, span], v_ref.at[:, span], e_sem.at[c])

    small = [
        pltpu.make_async_copy(src, dst, s_sem.at[i])
        for i, (src, dst) in enumerate(
            [(g_hbm, g_ref), (t_hbm, t_ref), (m_hbm, m_ref), (w_hbm, w_ref)]
        )
    ]
    small[0].start()
    small[1].start()
    for c in range(chunks):
        load(c).start()
    small[2].start()
    small[3].start()

    def each(low, high, fn):
        if high - low <= 8:
            for k in range(high - 1, low - 1, -1):
                fn(k)
        else:
            lax.fori_loop(low, high, lambda k, _: (fn(k), 0)[1], 0)

    barrier = pltpu.get_barrier_semaphore()

    def greet(to):
        pl.semaphore_signal(barrier, inc=1, device_id=to, device_id_type=MESH)

    each(1, n, lambda k: greet(snp_peer(k)))
    each(1, trait, lambda k: greet({"trait": jnp.bitwise_xor(mt, k)}))

    def copy(src, dst, c, phase, to):
        return pltpu.make_async_remote_copy(
            src_ref=src,
            dst_ref=dst,
            send_sem=out_sem.at[c, phase],
            recv_sem=in_sem.at[c, phase],
            device_id=to,
            device_id_type=MESH,
        )

    def drain(ref, sem):
        pltpu.make_async_copy(ref, ref, sem).wait()

    others = pl.ds(1, n - 1)
    rest = pl.ds(1, trait - 1)
    fewer = pl.ds(1, owners - 1)

    def sum_copy(c, o):
        to = base + o
        return copy(
            send[c].at[o], got[c].at[jnp.bitwise_xor(me, to)], c, 0, {"snp": to}
        )

    def own_copy(c, k):
        return copy(rg[c].at[mine], rg[c].at[mine], c, 1, snp_peer(k))

    def x_copy(c, k):
        return copy(gq[c].at[0], gq[c].at[k], c, 2, {"trait": jnp.bitwise_xor(mt, k)})

    def drain_owners(ref, sem):
        @pl.when(is_owner)
        def _():
            drain(ref.at[fewer], sem)

        @pl.when(jnp.logical_not(is_owner))
        def _():
            drain(ref, sem)

    small[0].wait()
    for h in range(groups):
        pick = one_hot_rows(owners, samples, per, h, 1.0)
        gs[h] = jnp.dot(pick, g_ref[...], preferred_element_type=F32).astype(BF16)
    held = samples // n
    small[1].wait()
    for h in range(groups):
        r = lax.broadcasted_iota(jnp.int32, (owners * SUB, held), 0)
        i = lax.broadcasted_iota(jnp.int32, (owners * SUB, held), 1)
        sample = me * held + i
        place = (sample // per) * SUB + h * per + lax.rem(sample, per)
        ts[h] = jnp.where(r == place, -1.0, 0.0).astype(BF16)

    def prepare_rows(_):
        for h in range(groups):
            pick = one_hot_rows(owners, samples, per, h, STEP)
            gt[h] = lax.dot_general(
                g_ref[...], pick, TT, preferred_element_type=F32
            ).astype(BF16)

    def prepare_level(level):
        if level == 0:
            small[2].wait()
            small[3].wait()
        shape = (trait * blocks, trait * blocks)
        a = lax.broadcasted_iota(jnp.int32, shape, 0)
        r = lax.broadcasted_iota(jnp.int32, shape, 1)
        slot = r // blocks
        there = jnp.bitwise_xor(slot, mt) * blocks + (r - slot * blocks)
        order = jnp.where(a == there, 1.0, 0.0).astype(BF16)
        member = m_ref[level].astype(F32)
        count = jnp.sum(member, axis=1, keepdims=True)
        placed = jnp.dot(
            member.astype(BF16), order, preferred_element_type=F32
        ).astype(BF16)
        weight = jnp.broadcast_to(w_ref[level : level + 1, :], (TB, member.shape[0])).T
        by_node = STEP * weight * jnp.sqrt(TB * jnp.maximum(count, 1.0))
        thr[level] = lax.dot_general(
            jnp.concatenate([placed] * 3, axis=0), split3(by_node), TN,
            preferred_element_type=F32,
        )
        ssum[level] = lax.dot_general(placed, placed, TN, preferred_element_type=F32).astype(BF16)

    kt = min(rows, 256)

    def fit(c):
        load(c).wait()
        total = jnp.zeros((owners * SUB, widths[c]), F32)
        for h in range(groups):
            total += jnp.dot(ts[h], t_ref[:, cols_of(c, h)], preferred_element_type=F32)
            for k in range(rows // kt):
                total += jnp.dot(
                    gs[h, :, k * kt : (k + 1) * kt],
                    v_ref[k * kt : (k + 1) * kt, cols_of(c, h)].astype(BF16),
                    preferred_element_type=F32,
                )
        send[c][...] = total.astype(BF16).reshape(owners, SUB, widths[c])
        if c == 0:
            pl.semaphore_wait(barrier, n + trait - 2)

        def give(o):
            @pl.when(me != base + o)
            def _():
                sum_copy(c, o).start()

        each(0, owners, give)

    def residual(c):
        @pl.when(is_owner)
        def _():
            drain(got[c].at[others], in_sem.at[c, 0])
            total = send[c][mine].astype(F32)
            total += jnp.sum(got[c][1:].astype(F32), axis=0)
            rg[c][mine] = (-total).astype(BF16)
            each(1, n, lambda k: own_copy(c, k).start())

    def value(c):
        w = widths[c]
        drain_owners(rg[c], in_sem.at[c, 1])
        resid = rg[c][...].reshape(owners * SUB, w)
        lane = lax.broadcasted_iota(jnp.int32, (rows, TB), 1)
        sums = jnp.zeros((rows, TB), F32)
        for h in range(groups):
            grad = jnp.dot(gt[h], resid, preferred_element_type=F32)
            moved = v_ref[:, cols_of(c, h)] + grad
            v_ref[:, cols_of(c, h)] = moved
            sq = moved * moved
            for b in range(w // TB):
                s = jnp.sum(sq[:, b * TB : (b + 1) * TB], axis=1, keepdims=True)
                sums = jnp.where(lane == h * (w // TB) + b, s, sums)
        gq[c][0] = sums.T[: groups * w // TB]
        each(1, trait, lambda k: x_copy(c, k).start())

    steps = {
        "fit": fit, "residual": residual, "value": value,
        "rows": prepare_rows, "level": prepare_level,
    }
    for step, c in plan:
        steps[step](c)

    for c in range(chunks):
        drain_owners(send[c], out_sem.at[c, 0])

        @pl.when(is_owner)
        def _():
            drain(got[c].at[others], out_sem.at[c, 1])

    for c in range(chunks):
        drain(gq[c].at[rest], in_sem.at[c, 2])

    block_sq = jnp.concatenate(
        [gq[c][k] for k in range(trait) for c in range(chunks)], axis=0
    )
    scale = None
    for level in range(levels):
        if level == 0:
            node_sq = block_sq
        else:
            node_sq = jnp.dot(
                jnp.concatenate([ssum[level]] * 3, axis=1),
                split3(block_sq),
                preferred_element_type=F32,
            )
        factor = jnp.maximum(1.0 - thr[level][:, :1] * lax.rsqrt(node_sq), 0.0)
        scale = factor[:blocks] if scale is None else scale * factor[:blocks]
        block_sq = block_sq * (factor * factor)
    sc_ref[:, :blocks] = scale.T
    for c in range(chunks):
        drain(gq[c].at[rest], out_sem.at[c, 2])


def scale_kernel(pieces, row_tile, v_ref, sc_ref, o_hbm, out, sem):
    rows, cols = v_ref.shape
    size = rows // pieces

    def store(p):
        r = pl.ds(pl.multiple_of(p * size, size), size)
        return pltpu.make_async_copy(out.at[r, :], o_hbm.at[r, :], sem.at[p])

    def piece(p, _):
        def tile(i, _):
            start = pl.multiple_of(p * size + i * row_tile, row_tile)
            r = pl.ds(start, row_tile)
            sc = sc_ref[r, :]
            for b in range(cols // TB):
                c = slice(b * TB, (b + 1) * TB)
                out[r, c] = v_ref[r, c] * sc[:, b : b + 1]
            return 0

        lax.fori_loop(0, size // row_tile, tile, 0)
        store(p).start()
        return 0

    lax.fori_loop(0, pieces, piece, 0)
    lax.fori_loop(0, pieces, lambda p, _: (store(p).wait(), 0)[1], 0)


def body(n, trait, genotype, targets, effect_sizes, membership, node_weight):
    samples, rows = genotype.shape
    cols = effect_sizes.shape[1]
    blocks = cols // TB
    levels = membership.shape[0]
    owners = n // 2
    groups = SUB * owners // samples
    lines = cols // groups
    widths = [lines * part // 8 for part in (2, 2, 2, 2)]
    chunks = len(widths)
    names = {"F": "fit", "D": "residual", "V": "value", "R": "rows", "L": "level"}
    order = ["F0", "R0", "F1", "L0", "L1", "F2", "L2", "L3", "F3"]
    order += ["D0", "D1", "D2", "D3", "V0", "V1", "V2", "V3"]
    plan = [(names[x[0]], int(x[1])) for x in order]
    vmem = pl.BlockSpec(memory_space=pltpu.VMEM)
    hbm = pl.BlockSpec(memory_space=pl.ANY)
    dma = pltpu.SemaphoreType.DMA
    value, scale = pl.pallas_call(
        functools.partial(fit_kernel, n, trait, widths, plan),
        name="fit",
        out_shape=(pltpu.VMEM((rows, cols), F32), pltpu.VMEM((rows, TB), F32)),
        in_specs=[hbm] * 5,
        out_specs=(vmem, vmem),
        scratch_shapes=[
            *[pltpu.VMEM((owners, SUB, w), BF16) for w in widths],
            *[pltpu.VMEM((n, SUB, w), BF16) for w in widths],
            *[pltpu.VMEM((owners, SUB, w), BF16) for w in widths],
            *[pltpu.VMEM((trait, groups * w // TB, rows), F32) for w in widths],
            pltpu.VMEM(genotype.shape, BF16),
            pltpu.VMEM(targets.shape, BF16),
            pltpu.VMEM(membership.shape, jnp.int32),
            pltpu.VMEM(node_weight.shape, F32),
            pltpu.VMEM((groups, owners * SUB, samples // n), BF16),
            pltpu.VMEM((groups, owners * SUB, rows), BF16),
            pltpu.VMEM((groups, rows, owners * SUB), BF16),
            pltpu.VMEM((levels, trait * blocks, trait * blocks), BF16),
            pltpu.VMEM((levels, trait * blocks, TB), F32),
            dma((4,)),
            dma((chunks,)),
            dma((chunks, 3)),
            dma((chunks, 3)),
        ],
        compiler_params=pltpu.CompilerParams(
            collective_id=0, has_side_effects=True, vmem_limit_bytes=40 << 20
        ),
    )(genotype, targets, membership, node_weight, effect_sizes)
    value = pltpu.with_memory_space_constraint(value, pltpu.VMEM)
    scale = pltpu.with_memory_space_constraint(scale, pltpu.VMEM)
    pieces = 8
    return pl.pallas_call(
        functools.partial(scale_kernel, pieces, min(rows // pieces, 128)),
        name="scale",
        out_shape=jax.ShapeDtypeStruct((rows, cols), F32),
        in_specs=[vmem, vmem],
        out_specs=hbm,
        scratch_shapes=[pltpu.VMEM((rows, cols), F32), dma((pieces,))],
        compiler_params=pltpu.CompilerParams(vmem_limit_bytes=40 << 20),
    )(value, scale)


def solution(mesh):
    n, trait = mesh.shape["snp"], mesh.shape["trait"]
    return jax.shard_map(
        functools.partial(body, n, trait),
        mesh=mesh,
        in_specs=(P(None, "snp"), P("snp", "trait"), P("snp", "trait"), P(), P()),
        out_specs=P("snp", "trait"),
        check_vma=False,
    )
```

```python
import functools

import jax
import jax.numpy as jnp
from jax import lax
from jax.experimental import pallas as pl
from jax.experimental.pallas import tpu as pltpu
from jax.sharding import PartitionSpec as P

TB = 128
SUB = 16
STEP = 0.5
F32 = jnp.float32
BF16 = jnp.bfloat16
MESH = pl.DeviceIdType.MESH
TN = (((0,), (0,)), ((), ()))


def one_hot_rows(slots, samples, per, group, gain):
    r = lax.broadcasted_iota(jnp.int32, (slots * SUB, samples), 0)
    n = lax.broadcasted_iota(jnp.int32, (slots * SUB, samples), 1)
    owner = lax.shift_right_logical(r, 4)
    inner = jnp.bitwise_and(r, SUB - 1) - group * per
    hit = (n == owner * per + inner) & (inner >= 0) & (inner < per)
    return jnp.where(hit, gain, 0.0).astype(BF16)


def split3(x):
    hi = x.astype(BF16)
    x = x - hi.astype(F32)
    mid = x.astype(BF16)
    low = (x - mid.astype(F32)).astype(BF16)
    return [hi, mid, low]


def fit_kernel(
    n, trait, widths, plan,
    g_hbm, t_hbm, m_hbm, w_hbm, e_hbm,
    v_ref, sc_ref, *scratch,
):
    chunks = len(widths)
    send, got, rg, gq = (scratch[i * chunks : (i + 1) * chunks] for i in range(4))
    g_ref, t_ref, m_ref, w_ref, ts, gs, gt, ssum, thr, s_sem, e_sem, out_sem, in_sem = scratch[4 * chunks :]
    me = lax.axis_index("snp")
    mt = lax.axis_index("trait")
    samples, rows = g_ref.shape
    owners = n // 2
    base = n // 4
    per = samples // owners
    groups = SUB // per
    mine = me - base
    is_owner = (mine >= 0) & (mine < owners)
    cols = v_ref.shape[1]
    blocks = cols // TB
    levels = m_ref.shape[0]
    first = [sum(widths[:c]) for c in range(chunks)]

    def snp_peer(slot):
        return {"snp": jnp.bitwise_xor(me, slot)}

    def cols_of(c, h):
        return pl.ds(groups * first[c] + h * widths[c], widths[c])

    def load(c):
        span = pl.ds(groups * first[c], groups * widths[c])
        return pltpu.make_async_copy(e_hbm.at[:, span], v_ref.at[:, span], e_sem.at[c])

    small = [
        pltpu.make_async_copy(src, dst, s_sem.at[i])
        for i, (src, dst) in enumerate(
            [(g_hbm, g_ref), (t_hbm, t_ref), (m_hbm, m_ref), (w_hbm, w_ref)]
        )
    ]
    small[0].start()
    small[1].start()
    for c in range(chunks):
        load(c).start()
    small[2].start()
    small[3].start()

    def each(low, high, fn):
        if high - low <= 8:
            for k in range(high - 1, low - 1, -1):
                fn(k)
        else:
            lax.fori_loop(low, high, lambda k, _: (fn(k), 0)[1], 0)

    barrier = pltpu.get_barrier_semaphore()

    def greet(to):
        pl.semaphore_signal(barrier, inc=1, device_id=to, device_id_type=MESH)

    each(1, n, lambda k: greet(snp_peer(k)))
    each(1, trait, lambda k: greet({"trait": jnp.bitwise_xor(mt, k)}))

    def copy(src, dst, c, phase, to):
        return pltpu.make_async_remote_copy(
            src_ref=src,
            dst_ref=dst,
            send_sem=out_sem.at[c, phase],
            recv_sem=in_sem.at[c, phase],
            device_id=to,
            device_id_type=MESH,
        )

    def drain(ref, sem):
        pltpu.make_async_copy(ref, ref, sem).wait()

    others = pl.ds(1, n - 1)
    rest = pl.ds(1, trait - 1)
    fewer = pl.ds(1, owners - 1)

    def sum_copy(c, o):
        to = base + o
        return copy(
            send[c].at[o], got[c].at[jnp.bitwise_xor(me, to)], c, 0, {"snp": to}
        )

    def own_copy(c, k):
        return copy(rg[c].at[mine], rg[c].at[mine], c, 1, snp_peer(k))

    def x_copy(c, k):
        return copy(gq[c].at[0], gq[c].at[k], c, 2, {"trait": jnp.bitwise_xor(mt, k)})

    def drain_owners(ref, sem):
        @pl.when(is_owner)
        def _():
            drain(ref.at[fewer], sem)

        @pl.when(jnp.logical_not(is_owner))
        def _():
            drain(ref, sem)

    small[0].wait()
    for h in range(groups):
        pick = one_hot_rows(owners, samples, per, h, 1.0)
        gs[h] = jnp.dot(pick, g_ref[...], preferred_element_type=F32).astype(BF16)
    held = samples // n
    small[1].wait()
    for h in range(groups):
        r = lax.broadcasted_iota(jnp.int32, (owners * SUB, held), 0)
        i = lax.broadcasted_iota(jnp.int32, (owners * SUB, held), 1)
        sample = me * held + i
        place = (sample // per) * SUB + h * per + lax.rem(sample, per)
        ts[h] = jnp.where(r == place, -1.0, 0.0).astype(BF16)

    def prepare_rows(_):
        for h in range(groups):
            gt[h] = (gs[h].astype(F32).T * STEP).astype(BF16)

    def prepare_levels(_):
        small[2].wait()
        small[3].wait()
        nodes = trait * blocks
        a = lax.broadcasted_iota(jnp.int32, (nodes, nodes), 0)
        r = lax.broadcasted_iota(jnp.int32, (nodes, nodes), 1)
        slot = r // blocks
        there = jnp.bitwise_xor(slot, mt) * blocks + (r - slot * blocks)
        order = jnp.where(a == there, 1.0, 0.0).astype(BF16)
        weight = jnp.concatenate([w_ref[...]] * (8 // levels), axis=0).T
        lines = []
        for level in range(levels):
            member = m_ref[level].astype(F32)
            count = jnp.sum(member, axis=1, keepdims=True)
            placed = jnp.dot(member.astype(BF16), order, preferred_element_type=F32)
            by_node = (
                STEP * weight[:, level : level + 1] * jnp.sqrt(TB * jnp.maximum(count, 1.0))
            )
            lines.append(jnp.sum(placed * by_node, axis=0, keepdims=True))
            near = placed.astype(BF16)
            ssum[level] = lax.dot_general(
                near, near, TN, preferred_element_type=F32
            ).astype(BF16)
        thr[...] = jnp.concatenate(lines * (8 // levels), axis=0).T

    kt = min(rows, 256)

    def fit(c):
        load(c).wait()
        total = jnp.zeros((owners * SUB, widths[c]), F32)
        for h in range(groups):
            total += jnp.dot(ts[h], t_ref[:, cols_of(c, h)], preferred_element_type=F32)
            for k in range(rows // kt):
                total += jnp.dot(
                    gs[h, :, k * kt : (k + 1) * kt],
                    v_ref[k * kt : (k + 1) * kt, cols_of(c, h)].astype(BF16),
                    preferred_element_type=F32,
                )
        send[c][...] = total.astype(BF16).reshape(owners, SUB, widths[c])
        if c == 0:
            pl.semaphore_wait(barrier, n + trait - 2)

        def give(j):
            o = jnp.bitwise_xor(lax.rem(me, owners), j)

            @pl.when(me != base + o)
            def _():
                sum_copy(c, o).start()

        each(0, owners, give)

    def residual(c):
        @pl.when(is_owner)
        def _():
            drain(got[c].at[others], in_sem.at[c, 0])
            total = send[c][mine].astype(F32)
            total += jnp.sum(got[c][1:].astype(F32), axis=0)
            rg[c][mine] = (-total).astype(BF16)
            each(1, n, lambda k: own_copy(c, k).start())

    def value(c):
        w = widths[c]
        drain_owners(rg[c], in_sem.at[c, 1])
        resid = rg[c][...].reshape(owners * SUB, w)
        lane = lax.broadcasted_iota(jnp.int32, (rows, TB), 1)
        sums = jnp.zeros((rows, TB), F32)
        for h in range(groups):
            grad = jnp.dot(gt[h], resid, preferred_element_type=F32)
            moved = v_ref[:, cols_of(c, h)] + grad
            v_ref[:, cols_of(c, h)] = moved
            sq = moved * moved
            for b in range(w // TB):
                s = jnp.sum(sq[:, b * TB : (b + 1) * TB], axis=1, keepdims=True)
                sums = jnp.where(lane == h * (w // TB) + b, s, sums)
        gq[c][0] = sums.T[: groups * w // TB]
        each(1, trait, lambda k: x_copy(c, k).start())

    steps = {
        "fit": fit, "residual": residual, "value": value,
        "rows": prepare_rows, "levels": prepare_levels,
    }
    for step, c in plan:
        steps[step](c)

    for c in range(chunks):
        drain_owners(send[c], out_sem.at[c, 0])

        @pl.when(is_owner)
        def _():
            drain(got[c].at[others], out_sem.at[c, 1])

    for c in range(chunks):
        drain(gq[c].at[rest], in_sem.at[c, 2])

    block_sq = jnp.concatenate(
        [gq[c][k] for k in range(trait) for c in range(chunks)], axis=0
    )
    limits = thr[...]
    scale = None
    for level in range(levels):
        if level == 0:
            node_sq = block_sq
        else:
            node_sq = jnp.dot(
                jnp.concatenate([ssum[level]] * 3, axis=1),
                jnp.concatenate(split3(block_sq), axis=0),
                preferred_element_type=F32,
            )
        factor = jnp.maximum(1.0 - limits[:, level : level + 1] * lax.rsqrt(node_sq), 0.0)
        scale = factor[:blocks] if scale is None else scale * factor[:blocks]
        block_sq = block_sq * (factor * factor)
    sc_ref[...] = scale
    for c in range(chunks):
        drain(gq[c].at[rest], out_sem.at[c, 2])


def scale_kernel(spans, v_ref, sc_ref, o_hbm, out, sem):
    rows = v_ref.shape[0]
    blocks = sc_ref.shape[0]
    parts = [x.astype(F32) for x in split3(sc_ref[...])]
    terms = jnp.concatenate(parts, axis=0).T.astype(BF16)

    def store(p):
        c = pl.ds(*spans[p])
        return pltpu.make_async_copy(out.at[:, c], o_hbm.at[:, c], sem.at[p])

    for p, (first, width) in enumerate(spans):
        k = lax.broadcasted_iota(jnp.int32, (3 * blocks, width), 0)
        c = lax.broadcasted_iota(jnp.int32, (3 * blocks, width), 1)
        hit = lax.rem(k, blocks) == (first + c) // TB
        spread = jnp.where(hit, 1.0, 0.0).astype(BF16)
        factor = jnp.dot(terms, spread, preferred_element_type=F32)
        c = pl.ds(first, width)
        out[:, c] = v_ref[:, c] * factor
        store(p).start()
    for p in range(len(spans)):
        store(p).wait()


def body(n, trait, genotype, targets, effect_sizes, membership, node_weight):
    samples, rows = genotype.shape
    cols = effect_sizes.shape[1]
    blocks = cols // TB
    levels = membership.shape[0]
    owners = n // 2
    groups = SUB * owners // samples
    lines = cols // groups
    widths = [lines * part // 8 for part in (2, 2, 2, 2)]
    chunks = len(widths)
    names = {"F": "fit", "D": "residual", "V": "value", "R": "rows", "L": "levels"}
    order = ["F0", "F1", "F2", "F3", "R0", "D0", "D1", "L0"]
    order += ["D2", "D3", "V0", "V1", "V2", "V3"]
    plan = [(names[x[0]], int(x[1])) for x in order]
    vmem = pl.BlockSpec(memory_space=pltpu.VMEM)
    hbm = pl.BlockSpec(memory_space=pl.ANY)
    dma = pltpu.SemaphoreType.DMA
    value, scale = pl.pallas_call(
        functools.partial(fit_kernel, n, trait, widths, plan),
        name="fit",
        out_shape=(pltpu.VMEM((rows, cols), F32), pltpu.VMEM((blocks, rows), F32)),
        in_specs=[hbm] * 5,
        out_specs=(vmem, vmem),
        scratch_shapes=[
            *[pltpu.VMEM((owners, SUB, w), BF16) for w in widths],
            *[pltpu.VMEM((n, SUB, w), BF16) for w in widths],
            *[pltpu.VMEM((owners, SUB, w), BF16) for w in widths],
            *[pltpu.VMEM((trait, groups * w // TB, rows), F32) for w in widths],
            pltpu.VMEM(genotype.shape, BF16),
            pltpu.VMEM(targets.shape, BF16),
            pltpu.VMEM(membership.shape, jnp.int32),
            pltpu.VMEM(node_weight.shape, F32),
            pltpu.VMEM((groups, owners * SUB, samples // n), BF16),
            pltpu.VMEM((groups, owners * SUB, rows), BF16),
            pltpu.VMEM((groups, rows, owners * SUB), BF16),
            pltpu.VMEM((levels, trait * blocks, trait * blocks), BF16),
            pltpu.VMEM((trait * blocks, 8), F32),
            dma((4,)),
            dma((chunks,)),
            dma((chunks, 3)),
            dma((chunks, 3)),
        ],
        compiler_params=pltpu.CompilerParams(
            collective_id=0, has_side_effects=True, vmem_limit_bytes=40 << 20
        ),
    )(genotype, targets, membership, node_weight, effect_sizes)
    value = pltpu.with_memory_space_constraint(value, pltpu.VMEM)
    scale = pltpu.with_memory_space_constraint(scale, pltpu.VMEM)
    sizes = [cols // 16] * 2 + [cols // 8] * 7
    spans = [(sum(sizes[:p]), size) for p, size in enumerate(sizes)]
    return pl.pallas_call(
        functools.partial(scale_kernel, spans),
        name="scale",
        out_shape=jax.ShapeDtypeStruct((rows, cols), F32),
        in_specs=[vmem, vmem],
        out_specs=hbm,
        scratch_shapes=[pltpu.VMEM((rows, cols), F32), dma((len(sizes),))],
        compiler_params=pltpu.CompilerParams(vmem_limit_bytes=40 << 20),
    )(value, scale)


def solution(mesh):
    n, trait = mesh.shape["snp"], mesh.shape["trait"]
    return jax.shard_map(
        functools.partial(body, n, trait),
        mesh=mesh,
        in_specs=(P(None, "snp"), P("snp", "trait"), P("snp", "trait"), P(), P()),
        out_specs=P("snp", "trait"),
        check_vma=False,
    )
```

```python
import functools

import jax
import jax.numpy as jnp
from jax import lax
from jax.experimental import pallas as pl
from jax.experimental.pallas import tpu as pltpu
from jax.sharding import PartitionSpec as P

TB = 128
SUB = 16
STEP = 0.5
F32 = jnp.float32
BF16 = jnp.bfloat16
MESH = pl.DeviceIdType.MESH
TN = (((0,), (0,)), ((), ()))


def one_hot_rows(slots, samples, per, group, gain):
    r = lax.broadcasted_iota(jnp.int32, (slots * SUB, samples), 0)
    n = lax.broadcasted_iota(jnp.int32, (slots * SUB, samples), 1)
    owner = lax.shift_right_logical(r, 4)
    inner = jnp.bitwise_and(r, SUB - 1) - group * per
    hit = (n == owner * per + inner) & (inner >= 0) & (inner < per)
    return jnp.where(hit, gain, 0.0).astype(BF16)


def split3(x):
    hi = x.astype(BF16)
    x = x - hi.astype(F32)
    mid = x.astype(BF16)
    low = (x - mid.astype(F32)).astype(BF16)
    return [hi, mid, low]


def fit_kernel(
    n, trait, widths, plan,
    g_hbm, t_hbm, m_hbm, w_hbm, e_hbm,
    v_ref, sc_ref, *scratch,
):
    chunks = len(widths)
    send, got, rg, gq = (scratch[i * chunks : (i + 1) * chunks] for i in range(4))
    g_ref, t_ref, m_ref, w_ref, ts, gs, gt, ssum, thr, s_sem, e_sem, out_sem, in_sem = scratch[4 * chunks :]
    me = lax.axis_index("snp")
    mt = lax.axis_index("trait")
    samples, rows = g_ref.shape
    owners = n // 2
    base = n // 4
    per = samples // owners
    groups = SUB // per
    mine = me - base
    is_owner = (mine >= 0) & (mine < owners)
    cols = v_ref.shape[1]
    blocks = cols // TB
    levels = m_ref.shape[0]
    first = [sum(widths[:c]) for c in range(chunks)]

    def snp_peer(slot):
        return {"snp": jnp.bitwise_xor(me, slot)}

    def cols_of(c, h):
        return pl.ds(groups * first[c] + h * widths[c], widths[c])

    def load(c):
        span = pl.ds(groups * first[c], groups * widths[c])
        return pltpu.make_async_copy(e_hbm.at[:, span], v_ref.at[:, span], e_sem.at[c])

    small = [
        pltpu.make_async_copy(src, dst, s_sem.at[i])
        for i, (src, dst) in enumerate(
            [(g_hbm, g_ref), (t_hbm, t_ref), (m_hbm, m_ref), (w_hbm, w_ref)]
        )
    ]
    small[0].start()
    small[1].start()
    for c in range(chunks):
        load(c).start()
    small[2].start()
    small[3].start()

    def each(low, high, fn, up=False):
        if high - low <= 8:
            for k in range(low, high) if up else range(high - 1, low - 1, -1):
                fn(k)
        else:
            lax.fori_loop(low, high, lambda k, _: (fn(k), 0)[1], 0)

    barrier = pltpu.get_barrier_semaphore()

    def greet(to):
        pl.semaphore_signal(barrier, inc=1, device_id=to, device_id_type=MESH)

    each(1, n, lambda k: greet(snp_peer(k)))
    each(1, trait, lambda k: greet({"trait": jnp.bitwise_xor(mt, k)}))

    def copy(src, dst, c, phase, to):
        return pltpu.make_async_remote_copy(
            src_ref=src,
            dst_ref=dst,
            send_sem=out_sem.at[c, phase],
            recv_sem=in_sem.at[c, phase],
            device_id=to,
            device_id_type=MESH,
        )

    def drain(ref, sem):
        pltpu.make_async_copy(ref, ref, sem).wait()

    others = pl.ds(1, n - 1)
    rest = pl.ds(1, trait - 1)
    fewer = pl.ds(1, owners - 1)

    def sum_copy(c, o):
        to = base + o
        return copy(
            send[c].at[o], got[c].at[jnp.bitwise_xor(me, to)], c, 0, {"snp": to}
        )

    def own_copy(c, k):
        return copy(rg[c].at[mine], rg[c].at[mine], c, 1, snp_peer(k))

    def x_copy(c, k):
        return copy(gq[c].at[0], gq[c].at[k], c, 2, {"trait": jnp.bitwise_xor(mt, k)})

    def drain_owners(ref, sem):
        @pl.when(is_owner)
        def _():
            drain(ref.at[fewer], sem)

        @pl.when(jnp.logical_not(is_owner))
        def _():
            drain(ref, sem)

    small[0].wait()
    for h in range(groups):
        pick = one_hot_rows(owners, samples, per, h, 1.0)
        gs[h] = jnp.dot(pick, g_ref[...], preferred_element_type=F32).astype(BF16)
    held = samples // n
    small[1].wait()
    for h in range(groups):
        r = lax.broadcasted_iota(jnp.int32, (owners * SUB, held), 0)
        i = lax.broadcasted_iota(jnp.int32, (owners * SUB, held), 1)
        sample = me * held + i
        place = (sample // per) * SUB + h * per + lax.rem(sample, per)
        ts[h] = jnp.where(r == place, -1.0, 0.0).astype(BF16)

    def prepare_rows(_):
        for h in range(groups):
            gt[h] = (gs[h].astype(F32).T * STEP).astype(BF16)

    def prepare_levels(_):
        small[2].wait()
        small[3].wait()
        nodes = trait * blocks
        a = lax.broadcasted_iota(jnp.int32, (nodes, nodes), 0)
        r = lax.broadcasted_iota(jnp.int32, (nodes, nodes), 1)
        slot = r // blocks
        there = jnp.bitwise_xor(slot, mt) * blocks + (r - slot * blocks)
        order = jnp.where(a == there, 1.0, 0.0).astype(BF16)
        weight = jnp.concatenate([w_ref[...]] * (8 // levels), axis=0).T
        lines = []
        for level in range(levels):
            member = m_ref[level].astype(F32)
            count = jnp.sum(member, axis=1, keepdims=True)
            placed = jnp.dot(member.astype(BF16), order, preferred_element_type=F32)
            by_node = (
                STEP * weight[:, level : level + 1] * jnp.sqrt(TB * jnp.maximum(count, 1.0))
            )
            lines.append(jnp.sum(placed * by_node, axis=0, keepdims=True))
            near = placed.astype(BF16)
            ssum[level] = lax.dot_general(
                near, near, TN, preferred_element_type=F32
            ).astype(BF16)
        thr[...] = jnp.concatenate(lines * (8 // levels), axis=0).T

    kt = min(rows, 256)

    def fit(c):
        load(c).wait()
        total = jnp.zeros((owners * SUB, widths[c]), F32)
        for h in range(groups):
            total += jnp.dot(ts[h], t_ref[:, cols_of(c, h)], preferred_element_type=F32)
            for k in range(rows // kt):
                total += jnp.dot(
                    gs[h, :, k * kt : (k + 1) * kt],
                    v_ref[k * kt : (k + 1) * kt, cols_of(c, h)].astype(BF16),
                    preferred_element_type=F32,
                )
        send[c][...] = total.astype(BF16).reshape(owners, SUB, widths[c])
        if c == 0:
            pl.semaphore_wait(barrier, n + trait - 2)

        def give(j):
            o = jnp.bitwise_xor(lax.rem(me, owners), j)

            @pl.when(me != base + o)
            def _():
                sum_copy(c, o).start()

        each(0, owners, give)

    def residual(c):
        @pl.when(is_owner)
        def _():
            drain(got[c].at[others], in_sem.at[c, 0])
            total = send[c][mine].astype(F32)
            total += jnp.sum(got[c][1:].astype(F32), axis=0)
            rg[c][mine] = (-total).astype(BF16)
            each(1, n, lambda k: own_copy(c, k).start(), up=True)

    def value(c):
        w = widths[c]
        drain_owners(rg[c], in_sem.at[c, 1])
        resid = rg[c][...].reshape(owners * SUB, w)
        lane = lax.broadcasted_iota(jnp.int32, (rows, TB), 1)
        sums = jnp.zeros((rows, TB), F32)
        for h in range(groups):
            grad = jnp.dot(gt[h], resid, preferred_element_type=F32)
            moved = v_ref[:, cols_of(c, h)] + grad
            v_ref[:, cols_of(c, h)] = moved
            sq = moved * moved
            for b in range(w // TB):
                s = jnp.sum(sq[:, b * TB : (b + 1) * TB], axis=1, keepdims=True)
                sums = jnp.where(lane == h * (w // TB) + b, s, sums)
        gq[c][0] = sums.T[: groups * w // TB]
        each(1, trait, lambda k: x_copy(c, k).start(), up=True)

    steps = {
        "fit": fit, "residual": residual, "value": value,
        "rows": prepare_rows, "levels": prepare_levels,
    }
    for step, c in plan:
        steps[step](c)

    for c in range(chunks):
        drain_owners(send[c], out_sem.at[c, 0])

        @pl.when(is_owner)
        def _():
            drain(got[c].at[others], out_sem.at[c, 1])

    for c in range(chunks):
        drain(gq[c].at[rest], in_sem.at[c, 2])

    block_sq = jnp.concatenate(
        [gq[c][k] for k in range(trait) for c in range(chunks)], axis=0
    )
    limits = thr[...]
    scale = None
    for level in range(levels):
        if level == 0:
            node_sq = block_sq
        else:
            node_sq = jnp.dot(
                jnp.concatenate([ssum[level]] * 3, axis=1),
                jnp.concatenate(split3(block_sq), axis=0),
                preferred_element_type=F32,
            )
        factor = jnp.maximum(1.0 - limits[:, level : level + 1] * lax.rsqrt(node_sq), 0.0)
        scale = factor[:blocks] if scale is None else scale * factor[:blocks]
        block_sq = block_sq * (factor * factor)
    sc_ref[...] = scale
    for c in range(chunks):
        drain(gq[c].at[rest], out_sem.at[c, 2])


def scale_kernel(spans, v_ref, sc_ref, o_hbm, out, sem):
    rows = v_ref.shape[0]
    blocks = sc_ref.shape[0]
    parts = [x.astype(F32) for x in split3(sc_ref[...])]
    terms = jnp.concatenate(parts, axis=0).T.astype(BF16)

    def store(p):
        c = pl.ds(*spans[p])
        return pltpu.make_async_copy(out.at[:, c], o_hbm.at[:, c], sem.at[p])

    for p, (first, width) in enumerate(spans):
        k = lax.broadcasted_iota(jnp.int32, (3 * blocks, width), 0)
        c = lax.broadcasted_iota(jnp.int32, (3 * blocks, width), 1)
        hit = lax.rem(k, blocks) == (first + c) // TB
        spread = jnp.where(hit, 1.0, 0.0).astype(BF16)
        factor = jnp.dot(terms, spread, preferred_element_type=F32)
        c = pl.ds(first, width)
        out[:, c] = v_ref[:, c] * factor
        store(p).start()
    for p in range(len(spans)):
        store(p).wait()


def body(n, trait, genotype, targets, effect_sizes, membership, node_weight):
    samples, rows = genotype.shape
    cols = effect_sizes.shape[1]
    blocks = cols // TB
    levels = membership.shape[0]
    owners = n // 2
    groups = SUB * owners // samples
    lines = cols // groups
    widths = [lines * part // 8 for part in (2, 2, 2, 2)]
    chunks = len(widths)
    names = {"F": "fit", "D": "residual", "V": "value", "R": "rows", "L": "levels"}
    order = ["F0", "F1", "F2", "F3", "R0", "D0", "D1", "L0"]
    order += ["D2", "D3", "V0", "V1", "V2", "V3"]
    plan = [(names[x[0]], int(x[1])) for x in order]
    vmem = pl.BlockSpec(memory_space=pltpu.VMEM)
    hbm = pl.BlockSpec(memory_space=pl.ANY)
    dma = pltpu.SemaphoreType.DMA
    value, scale = pl.pallas_call(
        functools.partial(fit_kernel, n, trait, widths, plan),
        name="fit",
        out_shape=(pltpu.VMEM((rows, cols), F32), pltpu.VMEM((blocks, rows), F32)),
        in_specs=[hbm] * 5,
        out_specs=(vmem, vmem),
        scratch_shapes=[
            *[pltpu.VMEM((owners, SUB, w), BF16) for w in widths],
            *[pltpu.VMEM((n, SUB, w), BF16) for w in widths],
            *[pltpu.VMEM((owners, SUB, w), BF16) for w in widths],
            *[pltpu.VMEM((trait, groups * w // TB, rows), F32) for w in widths],
            pltpu.VMEM(genotype.shape, BF16),
            pltpu.VMEM(targets.shape, BF16),
            pltpu.VMEM(membership.shape, jnp.int32),
            pltpu.VMEM(node_weight.shape, F32),
            pltpu.VMEM((groups, owners * SUB, samples // n), BF16),
            pltpu.VMEM((groups, owners * SUB, rows), BF16),
            pltpu.VMEM((groups, rows, owners * SUB), BF16),
            pltpu.VMEM((levels, trait * blocks, trait * blocks), BF16),
            pltpu.VMEM((trait * blocks, 8), F32),
            dma((4,)),
            dma((chunks,)),
            dma((chunks, 3)),
            dma((chunks, 3)),
        ],
        compiler_params=pltpu.CompilerParams(
            collective_id=0, has_side_effects=True, vmem_limit_bytes=40 << 20
        ),
    )(genotype, targets, membership, node_weight, effect_sizes)
    value = pltpu.with_memory_space_constraint(value, pltpu.VMEM)
    scale = pltpu.with_memory_space_constraint(scale, pltpu.VMEM)
    sizes = [cols // 16] * 2 + [cols // 8] * 7
    spans = [(sum(sizes[:p]), size) for p, size in enumerate(sizes)]
    return pl.pallas_call(
        functools.partial(scale_kernel, spans),
        name="scale",
        out_shape=jax.ShapeDtypeStruct((rows, cols), F32),
        in_specs=[vmem, vmem],
        out_specs=hbm,
        scratch_shapes=[pltpu.VMEM((rows, cols), F32), dma((len(sizes),))],
        compiler_params=pltpu.CompilerParams(vmem_limit_bytes=40 << 20),
    )(value, scale)


def solution(mesh):
    n, trait = mesh.shape["snp"], mesh.shape["trait"]
    return jax.shard_map(
        functools.partial(body, n, trait),
        mesh=mesh,
        in_specs=(P(None, "snp"), P("snp", "trait"), P("snp", "trait"), P(), P()),
        out_specs=P("snp", "trait"),
        check_vma=False,
    )
```

```python
import functools

import jax
import jax.numpy as jnp
from jax import lax
from jax.experimental import pallas as pl
from jax.experimental.pallas import tpu as pltpu
from jax.sharding import PartitionSpec as P

TB = 128
SUB = 16
STEP = 0.5
F32 = jnp.float32
BF16 = jnp.bfloat16
MESH = pl.DeviceIdType.MESH
TN = (((0,), (0,)), ((), ()))


def one_hot_rows(slots, samples, per, group, gain):
    r = lax.broadcasted_iota(jnp.int32, (slots * SUB, samples), 0)
    n = lax.broadcasted_iota(jnp.int32, (slots * SUB, samples), 1)
    owner = lax.shift_right_logical(r, 4)
    inner = jnp.bitwise_and(r, SUB - 1) - group * per
    hit = (n == owner * per + inner) & (inner >= 0) & (inner < per)
    return jnp.where(hit, gain, 0.0).astype(BF16)


def split3(x):
    hi = x.astype(BF16)
    x = x - hi.astype(F32)
    mid = x.astype(BF16)
    low = (x - mid.astype(F32)).astype(BF16)
    return [hi, mid, low]


def fit_kernel(
    n, trait, widths, plan,
    g_hbm, t_hbm, m_hbm, w_hbm, e_hbm,
    v_ref, sc_ref, *scratch,
):
    chunks = len(widths)
    send, got, rg, gq = (scratch[i * chunks : (i + 1) * chunks] for i in range(4))
    g_ref, t_ref, m_ref, w_ref, ts, gs, gt, ssum, thr, s_sem, e_sem, out_sem, in_sem = scratch[4 * chunks :]
    me = lax.axis_index("snp")
    mt = lax.axis_index("trait")
    samples, rows = g_ref.shape
    owners = n // 2
    base = n // 4
    per = samples // owners
    groups = SUB // per
    mine = me - base
    is_owner = (mine >= 0) & (mine < owners)
    cols = v_ref.shape[1]
    blocks = cols // TB
    levels = m_ref.shape[0]
    first = [sum(widths[:c]) for c in range(chunks)]

    def snp_peer(slot):
        return {"snp": jnp.bitwise_xor(me, slot)}

    def cols_of(c, h):
        return pl.ds(groups * first[c] + h * widths[c], widths[c])

    def load(c):
        span = pl.ds(groups * first[c], groups * widths[c])
        return pltpu.make_async_copy(e_hbm.at[:, span], v_ref.at[:, span], e_sem.at[c])

    small = [
        pltpu.make_async_copy(src, dst, s_sem.at[i])
        for i, (src, dst) in enumerate(
            [(g_hbm, g_ref), (t_hbm, t_ref), (m_hbm, m_ref), (w_hbm, w_ref)]
        )
    ]
    small[0].start()
    small[1].start()
    for c in range(chunks):
        load(c).start()
    small[2].start()
    small[3].start()

    def each(low, high, fn, up=False):
        if high - low <= 8:
            for k in range(low, high) if up else range(high - 1, low - 1, -1):
                fn(k)
        else:
            lax.fori_loop(low, high, lambda k, _: (fn(k), 0)[1], 0)

    barrier = pltpu.get_barrier_semaphore()

    def greet(to):
        pl.semaphore_signal(barrier, inc=1, device_id=to, device_id_type=MESH)

    each(1, n, lambda k: greet(snp_peer(k)))
    each(1, trait, lambda k: greet({"trait": jnp.bitwise_xor(mt, k)}))

    def copy(src, dst, c, phase, to):
        return pltpu.make_async_remote_copy(
            src_ref=src,
            dst_ref=dst,
            send_sem=out_sem.at[c, phase],
            recv_sem=in_sem.at[c, phase],
            device_id=to,
            device_id_type=MESH,
        )

    def drain(ref, sem):
        pltpu.make_async_copy(ref, ref, sem).wait()

    others = pl.ds(1, n - 1)
    rest = pl.ds(1, trait - 1)
    fewer = pl.ds(1, owners - 1)

    def sum_copy(c, o):
        to = base + o
        return copy(
            send[c].at[o], got[c].at[jnp.bitwise_xor(me, to)], c, 0, {"snp": to}
        )

    def own_copy(c, k):
        return copy(rg[c].at[mine], rg[c].at[mine], c, 1, snp_peer(k))

    def x_copy(c, k):
        return copy(gq[c].at[0], gq[c].at[k], c, 2, {"trait": jnp.bitwise_xor(mt, k)})

    def drain_owners(ref, sem):
        @pl.when(is_owner)
        def _():
            drain(ref.at[fewer], sem)

        @pl.when(jnp.logical_not(is_owner))
        def _():
            drain(ref, sem)

    small[0].wait()
    for h in range(groups):
        pick = one_hot_rows(owners, samples, per, h, 1.0)
        gs[h] = jnp.dot(pick, g_ref[...], preferred_element_type=F32).astype(BF16)
    held = samples // n
    small[1].wait()
    for h in range(groups):
        r = lax.broadcasted_iota(jnp.int32, (owners * SUB, held), 0)
        i = lax.broadcasted_iota(jnp.int32, (owners * SUB, held), 1)
        sample = me * held + i
        place = (sample // per) * SUB + h * per + lax.rem(sample, per)
        ts[h] = jnp.where(r == place, -1.0, 0.0).astype(BF16)

    def prepare_rows(_):
        for h in range(groups):
            gt[h] = (gs[h].astype(F32).T * STEP).astype(BF16)

    def prepare_levels(_):
        small[2].wait()
        small[3].wait()
        nodes = trait * blocks
        a = lax.broadcasted_iota(jnp.int32, (nodes, nodes), 0)
        r = lax.broadcasted_iota(jnp.int32, (nodes, nodes), 1)
        slot = r // blocks
        there = jnp.bitwise_xor(slot, mt) * blocks + (r - slot * blocks)
        order = jnp.where(a == there, 1.0, 0.0).astype(BF16)
        weight = jnp.concatenate([w_ref[...]] * (8 // levels), axis=0).T
        lines = []
        for level in range(levels):
            member = m_ref[level].astype(F32)
            count = jnp.sum(member, axis=1, keepdims=True)
            placed = jnp.dot(member.astype(BF16), order, preferred_element_type=F32)
            by_node = (
                STEP * weight[:, level : level + 1] * jnp.sqrt(TB * jnp.maximum(count, 1.0))
            )
            lines.append(jnp.sum(placed * by_node, axis=0, keepdims=True))
            near = placed.astype(BF16)
            ssum[level] = lax.dot_general(
                near, near, TN, preferred_element_type=F32
            ).astype(BF16)
        thr[...] = jnp.concatenate(lines * (8 // levels), axis=0).T

    kt = min(rows, 512)

    def fit(c):
        load(c).wait()
        total = jnp.zeros((owners * SUB, widths[c]), F32)
        for h in range(groups):
            total += jnp.dot(ts[h], t_ref[:, cols_of(c, h)], preferred_element_type=F32)
            for k in range(rows // kt):
                total += jnp.dot(
                    gs[h, :, k * kt : (k + 1) * kt],
                    v_ref[k * kt : (k + 1) * kt, cols_of(c, h)].astype(BF16),
                    preferred_element_type=F32,
                )
        send[c][...] = total.astype(BF16).reshape(owners, SUB, widths[c])
        if c == 0:
            pl.semaphore_wait(barrier, n + trait - 2)

        def give(j):
            o = jnp.bitwise_xor(lax.rem(me, owners), j)

            @pl.when(me != base + o)
            def _():
                sum_copy(c, o).start()

        each(0, owners, give)

    def residual(c):
        @pl.when(is_owner)
        def _():
            drain(got[c].at[others], in_sem.at[c, 0])
            total = send[c][mine].astype(F32)
            total += jnp.sum(got[c][1:].astype(F32), axis=0)
            rg[c][mine] = (-total).astype(BF16)
            each(1, n, lambda k: own_copy(c, k).start(), up=True)

    def value(c):
        w = widths[c]
        drain_owners(rg[c], in_sem.at[c, 1])
        resid = rg[c][...].reshape(owners * SUB, w)
        lane = lax.broadcasted_iota(jnp.int32, (rows, TB), 1)
        sums = jnp.zeros((rows, TB), F32)
        for h in range(groups):
            grad = jnp.dot(gt[h], resid, preferred_element_type=F32)
            moved = v_ref[:, cols_of(c, h)] + grad
            v_ref[:, cols_of(c, h)] = moved
            sq = moved * moved
            for b in range(w // TB):
                s = jnp.sum(sq[:, b * TB : (b + 1) * TB], axis=1, keepdims=True)
                sums = jnp.where(lane == h * (w // TB) + b, s, sums)
        gq[c][0] = sums.T[: groups * w // TB]
        each(1, trait, lambda k: x_copy(c, k).start(), up=True)

    steps = {
        "fit": fit, "residual": residual, "value": value,
        "rows": prepare_rows, "levels": prepare_levels,
    }
    for step, c in plan:
        steps[step](c)

    for c in range(chunks):
        drain_owners(send[c], out_sem.at[c, 0])

        @pl.when(is_owner)
        def _():
            drain(got[c].at[others], out_sem.at[c, 1])

    for c in range(chunks):
        drain(gq[c].at[rest], in_sem.at[c, 2])

    block_sq = jnp.concatenate(
        [gq[c][k] for k in range(trait) for c in range(chunks)], axis=0
    )
    limits = thr[...]
    scale = None
    for level in range(levels):
        seen = blocks if level == levels - 1 else trait * blocks
        if level == 0:
            node_sq = block_sq[:seen]
        else:
            node_sq = jnp.dot(
                jnp.concatenate([ssum[level, :seen]] * 3, axis=1),
                jnp.concatenate(split3(block_sq), axis=0),
                preferred_element_type=F32,
            )
        limit = limits[:seen, level : level + 1]
        factor = jnp.maximum(1.0 - limit * lax.rsqrt(node_sq), 0.0)
        scale = factor[:blocks] if scale is None else scale * factor[:blocks]
        if level < levels - 1:
            block_sq = block_sq * (factor * factor)
    sc_ref[...] = scale
    for c in range(chunks):
        drain(gq[c].at[rest], out_sem.at[c, 2])


def scale_kernel(spans, v_ref, sc_ref, o_hbm, out, sem):
    rows = v_ref.shape[0]
    blocks = sc_ref.shape[0]
    parts = [x.astype(F32) for x in split3(sc_ref[...])]
    terms = jnp.concatenate(parts, axis=0).T.astype(BF16)

    def store(p):
        c = pl.ds(*spans[p])
        return pltpu.make_async_copy(out.at[:, c], o_hbm.at[:, c], sem.at[p])

    for p, (first, width) in enumerate(spans):
        k = lax.broadcasted_iota(jnp.int32, (3 * blocks, width), 0)
        c = lax.broadcasted_iota(jnp.int32, (3 * blocks, width), 1)
        hit = lax.rem(k, blocks) == (first + c) // TB
        spread = jnp.where(hit, 1.0, 0.0).astype(BF16)
        factor = jnp.dot(terms, spread, preferred_element_type=F32)
        c = pl.ds(first, width)
        out[:, c] = v_ref[:, c] * factor
        store(p).start()
    for p in range(len(spans)):
        store(p).wait()


def body(n, trait, genotype, targets, effect_sizes, membership, node_weight):
    samples, rows = genotype.shape
    cols = effect_sizes.shape[1]
    blocks = cols // TB
    levels = membership.shape[0]
    owners = n // 2
    groups = SUB * owners // samples
    lines = cols // groups
    widths = [lines * part // 8 for part in (2, 2, 2, 2)]
    chunks = len(widths)
    names = {"F": "fit", "D": "residual", "V": "value", "R": "rows", "L": "levels"}
    order = ["F0", "F1", "F2", "F3", "D0", "R0", "D1"]
    order += ["D2", "L0", "D3", "V0", "V1", "V2", "V3"]
    plan = [(names[x[0]], int(x[1])) for x in order]
    vmem = pl.BlockSpec(memory_space=pltpu.VMEM)
    hbm = pl.BlockSpec(memory_space=pl.ANY)
    dma = pltpu.SemaphoreType.DMA
    value, scale = pl.pallas_call(
        functools.partial(fit_kernel, n, trait, widths, plan),
        name="fit",
        out_shape=(pltpu.VMEM((rows, cols), F32), pltpu.VMEM((blocks, rows), F32)),
        in_specs=[hbm] * 5,
        out_specs=(vmem, vmem),
        scratch_shapes=[
            *[pltpu.VMEM((owners, SUB, w), BF16) for w in widths],
            *[pltpu.VMEM((n, SUB, w), BF16) for w in widths],
            *[pltpu.VMEM((owners, SUB, w), BF16) for w in widths],
            *[pltpu.VMEM((trait, groups * w // TB, rows), F32) for w in widths],
            pltpu.VMEM(genotype.shape, BF16),
            pltpu.VMEM(targets.shape, BF16),
            pltpu.VMEM(membership.shape, jnp.int32),
            pltpu.VMEM(node_weight.shape, F32),
            pltpu.VMEM((groups, owners * SUB, samples // n), BF16),
            pltpu.VMEM((groups, owners * SUB, rows), BF16),
            pltpu.VMEM((groups, rows, owners * SUB), BF16),
            pltpu.VMEM((levels, trait * blocks, trait * blocks), BF16),
            pltpu.VMEM((trait * blocks, 8), F32),
            dma((4,)),
            dma((chunks,)),
            dma((chunks, 3)),
            dma((chunks, 3)),
        ],
        compiler_params=pltpu.CompilerParams(
            collective_id=0, has_side_effects=True, vmem_limit_bytes=40 << 20
        ),
    )(genotype, targets, membership, node_weight, effect_sizes)
    value = pltpu.with_memory_space_constraint(value, pltpu.VMEM)
    scale = pltpu.with_memory_space_constraint(scale, pltpu.VMEM)
    sizes = [cols // 16] * 2 + [cols // 8] * 7
    spans = [(sum(sizes[:p]), size) for p, size in enumerate(sizes)]
    return pl.pallas_call(
        functools.partial(scale_kernel, spans),
        name="scale",
        out_shape=jax.ShapeDtypeStruct((rows, cols), F32),
        in_specs=[vmem, vmem],
        out_specs=hbm,
        scratch_shapes=[pltpu.VMEM((rows, cols), F32), dma((len(sizes),))],
        compiler_params=pltpu.CompilerParams(vmem_limit_bytes=40 << 20),
    )(value, scale)


def solution(mesh):
    n, trait = mesh.shape["snp"], mesh.shape["trait"]
    return jax.shard_map(
        functools.partial(body, n, trait),
        mesh=mesh,
        in_specs=(P(None, "snp"), P("snp", "trait"), P("snp", "trait"), P(), P()),
        out_specs=P("snp", "trait"),
        check_vma=False,
    )
```

```python
import functools

import jax
import jax.numpy as jnp
from jax import lax
from jax.experimental import pallas as pl
from jax.experimental.pallas import tpu as pltpu
from jax.sharding import PartitionSpec as P

TB = 128
SUB = 16
STEP = 0.5
F32 = jnp.float32
BF16 = jnp.bfloat16
MESH = pl.DeviceIdType.MESH
TN = (((0,), (0,)), ((), ()))


def one_hot_rows(slots, samples, per, group, gain):
    r = lax.broadcasted_iota(jnp.int32, (slots * SUB, samples), 0)
    n = lax.broadcasted_iota(jnp.int32, (slots * SUB, samples), 1)
    owner = lax.shift_right_logical(r, 4)
    inner = jnp.bitwise_and(r, SUB - 1) - group * per
    hit = (n == owner * per + inner) & (inner >= 0) & (inner < per)
    return jnp.where(hit, gain, 0.0).astype(BF16)


def split3(x):
    hi = x.astype(BF16)
    x = x - hi.astype(F32)
    mid = x.astype(BF16)
    low = (x - mid.astype(F32)).astype(BF16)
    return [hi, mid, low]


def fit_kernel(
    n, trait, widths, plan,
    g_hbm, t_hbm, m_hbm, w_hbm, e_hbm,
    v_ref, sc_ref, *scratch,
):
    chunks = len(widths)
    send, got, rg, gq = (scratch[i * chunks : (i + 1) * chunks] for i in range(4))
    g_ref, t_ref, m_ref, w_ref, ts, gs, gt, ssum, thr, s_sem, e_sem, out_sem, in_sem = scratch[4 * chunks :]
    me = lax.axis_index("snp")
    mt = lax.axis_index("trait")
    samples, rows = g_ref.shape
    owners = n // 2
    base = n // 4
    per = samples // owners
    groups = SUB // per
    mine = me - base
    is_owner = (mine >= 0) & (mine < owners)
    cols = v_ref.shape[1]
    blocks = cols // TB
    levels = m_ref.shape[0]
    first = [sum(widths[:c]) for c in range(chunks)]

    def snp_peer(slot):
        return {"snp": jnp.bitwise_xor(me, slot)}

    def cols_of(c, h):
        return pl.ds(groups * first[c] + h * widths[c], widths[c])

    def load(c):
        span = pl.ds(groups * first[c], groups * widths[c])
        return pltpu.make_async_copy(e_hbm.at[:, span], v_ref.at[:, span], e_sem.at[c])

    small = [
        pltpu.make_async_copy(src, dst, s_sem.at[i])
        for i, (src, dst) in enumerate(
            [(g_hbm, g_ref), (t_hbm, t_ref), (m_hbm, m_ref), (w_hbm, w_ref)]
        )
    ]
    small[0].start()
    small[1].start()
    for c in range(chunks):
        load(c).start()
    small[2].start()
    small[3].start()

    def each(low, high, fn, up=False):
        if high - low <= 8:
            for k in range(low, high) if up else range(high - 1, low - 1, -1):
                fn(k)
        else:
            lax.fori_loop(low, high, lambda k, _: (fn(k), 0)[1], 0)

    barrier = pltpu.get_barrier_semaphore()

    def greet(to):
        pl.semaphore_signal(barrier, inc=1, device_id=to, device_id_type=MESH)

    each(1, n, lambda k: greet(snp_peer(k)))
    each(1, trait, lambda k: greet({"trait": jnp.bitwise_xor(mt, k)}))

    def copy(src, dst, c, phase, to):
        return pltpu.make_async_remote_copy(
            src_ref=src,
            dst_ref=dst,
            send_sem=out_sem.at[c, phase],
            recv_sem=in_sem.at[c, phase],
            device_id=to,
            device_id_type=MESH,
        )

    def drain(ref, sem):
        pltpu.make_async_copy(ref, ref, sem).wait()

    others = pl.ds(1, n - 1)
    rest = pl.ds(1, trait - 1)
    fewer = pl.ds(1, owners - 1)

    def sum_copy(c, o):
        to = base + o
        return copy(
            send[c].at[o], got[c].at[jnp.bitwise_xor(me, to)], c, 0, {"snp": to}
        )

    def own_copy(c, k):
        return copy(rg[c].at[mine], rg[c].at[mine], c, 1, snp_peer(k))

    def x_copy(c, k):
        return copy(gq[c].at[0], gq[c].at[k], c, 2, {"trait": jnp.bitwise_xor(mt, k)})

    def drain_owners(ref, sem):
        @pl.when(is_owner)
        def _():
            drain(ref.at[fewer], sem)

        @pl.when(jnp.logical_not(is_owner))
        def _():
            drain(ref, sem)

    small[0].wait()
    for h in range(groups):
        pick = one_hot_rows(owners, samples, per, h, 1.0)
        gs[h] = jnp.dot(pick, g_ref[...], preferred_element_type=F32).astype(BF16)
    held = samples // n
    small[1].wait()
    for h in range(groups):
        r = lax.broadcasted_iota(jnp.int32, (owners * SUB, held), 0)
        i = lax.broadcasted_iota(jnp.int32, (owners * SUB, held), 1)
        sample = me * held + i
        place = (sample // per) * SUB + h * per + lax.rem(sample, per)
        ts[h] = jnp.where(r == place, -1.0, 0.0).astype(BF16)

    def prepare_rows(_):
        for h in range(groups):
            gt[h] = (gs[h].astype(F32).T * STEP).astype(BF16)

    def prepare_levels(_):
        small[2].wait()
        small[3].wait()
        nodes = trait * blocks
        a = lax.broadcasted_iota(jnp.int32, (nodes, nodes), 0)
        r = lax.broadcasted_iota(jnp.int32, (nodes, nodes), 1)
        slot = r // blocks
        there = jnp.bitwise_xor(slot, mt) * blocks + (r - slot * blocks)
        order = jnp.where(a == there, 1.0, 0.0).astype(BF16)
        weight = jnp.concatenate([w_ref[...]] * (8 // levels), axis=0).T
        lines = []
        for level in range(levels):
            member = m_ref[level].astype(F32)
            count = jnp.sum(member, axis=1, keepdims=True)
            placed = jnp.dot(member.astype(BF16), order, preferred_element_type=F32)
            by_node = (
                STEP * weight[:, level : level + 1] * jnp.sqrt(TB * jnp.maximum(count, 1.0))
            )
            lines.append(jnp.sum(placed * by_node, axis=0, keepdims=True))
            near = placed.astype(BF16)
            ssum[level] = lax.dot_general(
                near, near, TN, preferred_element_type=F32
            ).astype(BF16)
        thr[...] = jnp.concatenate(lines * (8 // levels), axis=0).T

    kt = min(rows, 512)

    def fit(c):
        load(c).wait()
        total = jnp.zeros((owners * SUB, widths[c]), F32)
        for h in range(groups):
            total += jnp.dot(ts[h], t_ref[:, cols_of(c, h)], preferred_element_type=F32)
            for k in range(rows // kt):
                total += jnp.dot(
                    gs[h, :, k * kt : (k + 1) * kt],
                    v_ref[k * kt : (k + 1) * kt, cols_of(c, h)].astype(BF16),
                    preferred_element_type=F32,
                )
        send[c][...] = total.astype(BF16).reshape(owners, SUB, widths[c])
        if c == 0:
            pl.semaphore_wait(barrier, n + trait - 2)

        def give(j):
            o = jnp.bitwise_xor(lax.rem(me, owners), j)

            @pl.when(me != base + o)
            def _():
                sum_copy(c, o).start()

        each(0, owners, give)

    def residual(c):
        @pl.when(is_owner)
        def _():
            drain(got[c].at[others], in_sem.at[c, 0])
            total = send[c][mine].astype(F32)
            total += jnp.sum(got[c][1:].astype(F32), axis=0)
            rg[c][mine] = (-total).astype(BF16)
            each(1, n, lambda k: own_copy(c, k).start(), up=True)

    def value(c):
        w = widths[c]
        drain_owners(rg[c], in_sem.at[c, 1])
        resid = rg[c][...].reshape(owners * SUB, w)
        lane = lax.broadcasted_iota(jnp.int32, (rows, TB), 1)
        sums = jnp.zeros((rows, TB), F32)
        for h in range(groups):
            grad = jnp.dot(gt[h], resid, preferred_element_type=F32)
            moved = v_ref[:, cols_of(c, h)] + grad
            v_ref[:, cols_of(c, h)] = moved
            sq = moved * moved
            for b in range(w // TB):
                s = jnp.sum(sq[:, b * TB : (b + 1) * TB], axis=1, keepdims=True)
                sums = jnp.where(lane == h * (w // TB) + b, s, sums)
        gq[c][0] = sums.T[: groups * w // TB]
        each(1, trait, lambda k: x_copy(c, k).start(), up=True)

    steps = {
        "fit": fit, "residual": residual, "value": value,
        "rows": prepare_rows, "levels": prepare_levels,
    }
    for step, c in plan:
        steps[step](c)

    for c in range(chunks):
        drain_owners(send[c], out_sem.at[c, 0])

        @pl.when(is_owner)
        def _():
            drain(got[c].at[others], out_sem.at[c, 1])

    for c in range(chunks):
        drain(gq[c].at[rest], in_sem.at[c, 2])

    block_sq = jnp.concatenate(
        [gq[c][k] for k in range(trait) for c in range(chunks)], axis=0
    )
    limits = thr[...]
    scale = None
    for level in range(levels):
        seen = blocks if level == levels - 1 else trait * blocks
        if level == 0:
            node_sq = block_sq[:seen]
        else:
            node_sq = jnp.dot(
                jnp.concatenate([ssum[level, :seen]] * 3, axis=1),
                jnp.concatenate(split3(block_sq), axis=0),
                preferred_element_type=F32,
            )
        limit = limits[:seen, level : level + 1]
        factor = jnp.maximum(1.0 - limit * lax.rsqrt(node_sq), 0.0)
        scale = factor[:blocks] if scale is None else scale * factor[:blocks]
        if level < levels - 1:
            block_sq = block_sq * (factor * factor)
    sc_ref[...] = scale
    for c in range(chunks):
        drain(gq[c].at[rest], out_sem.at[c, 2])


def scale_kernel(spans, v_ref, sc_ref, o_hbm, out, sem):
    rows = v_ref.shape[0]
    blocks = sc_ref.shape[0]
    parts = [x.astype(F32) for x in split3(sc_ref[...])]
    terms = jnp.concatenate(parts, axis=0).T.astype(BF16)

    def store(p):
        c = pl.ds(*spans[p])
        return pltpu.make_async_copy(out.at[:, c], o_hbm.at[:, c], sem.at[p])

    for p, (first, width) in enumerate(spans):
        k = lax.broadcasted_iota(jnp.int32, (3 * blocks, width), 0)
        c = lax.broadcasted_iota(jnp.int32, (3 * blocks, width), 1)
        hit = lax.rem(k, blocks) == (first + c) // TB
        spread = jnp.where(hit, 1.0, 0.0).astype(BF16)
        factor = jnp.dot(terms, spread, preferred_element_type=F32)
        c = pl.ds(first, width)
        out[:, c] = v_ref[:, c] * factor
        store(p).start()
    for p in range(len(spans)):
        store(p).wait()


def body(n, trait, genotype, targets, effect_sizes, membership, node_weight):
    samples, rows = genotype.shape
    cols = effect_sizes.shape[1]
    blocks = cols // TB
    levels = membership.shape[0]
    owners = n // 2
    groups = SUB * owners // samples
    lines = cols // groups
    widths = [lines * part // 8 for part in (2, 2, 2, 2)]
    chunks = len(widths)
    names = {"F": "fit", "D": "residual", "V": "value", "R": "rows", "L": "levels"}
    order = ["F0", "F1", "F2", "F3", "D0", "R0", "D1"]
    order += ["D2", "L0", "D3", "V0", "V1", "V2", "V3"]
    plan = [(names[x[0]], int(x[1])) for x in order]
    vmem = pl.BlockSpec(memory_space=pltpu.VMEM)
    hbm = pl.BlockSpec(memory_space=pl.ANY)
    dma = pltpu.SemaphoreType.DMA
    value, scale = pl.pallas_call(
        functools.partial(fit_kernel, n, trait, widths, plan),
        name="fit",
        out_shape=(pltpu.VMEM((rows, cols), F32), pltpu.VMEM((blocks, rows), F32)),
        in_specs=[hbm] * 5,
        out_specs=(vmem, vmem),
        scratch_shapes=[
            *[pltpu.VMEM((owners, SUB, w), BF16) for w in widths],
            *[pltpu.VMEM((n, SUB, w), BF16) for w in widths],
            *[pltpu.VMEM((owners, SUB, w), BF16) for w in widths],
            *[pltpu.VMEM((trait, groups * w // TB, rows), F32) for w in widths],
            pltpu.VMEM(genotype.shape, BF16),
            pltpu.VMEM(targets.shape, BF16),
            pltpu.VMEM(membership.shape, jnp.int32),
            pltpu.VMEM(node_weight.shape, F32),
            pltpu.VMEM((groups, owners * SUB, samples // n), BF16),
            pltpu.VMEM((groups, owners * SUB, rows), BF16),
            pltpu.VMEM((groups, rows, owners * SUB), BF16),
            pltpu.VMEM((levels, trait * blocks, trait * blocks), BF16),
            pltpu.VMEM((trait * blocks, 8), F32),
            dma((4,)),
            dma((chunks,)),
            dma((chunks, 3)),
            dma((chunks, 3)),
        ],
        compiler_params=pltpu.CompilerParams(
            collective_id=0, has_side_effects=True, vmem_limit_bytes=40 << 20
        ),
    )(genotype, targets, membership, node_weight, effect_sizes)
    value = pltpu.with_memory_space_constraint(value, pltpu.VMEM)
    scale = pltpu.with_memory_space_constraint(scale, pltpu.VMEM)
    sizes = [cols // 32] * 2 + [cols // 16] + [cols // 8] * 3 + [cols // 4] * 2
    spans = [(sum(sizes[:p]), size) for p, size in enumerate(sizes)]
    return pl.pallas_call(
        functools.partial(scale_kernel, spans),
        name="scale",
        out_shape=jax.ShapeDtypeStruct((rows, cols), F32),
        in_specs=[vmem, vmem],
        out_specs=hbm,
        scratch_shapes=[pltpu.VMEM((rows, cols), F32), dma((len(sizes),))],
        compiler_params=pltpu.CompilerParams(vmem_limit_bytes=40 << 20),
    )(value, scale)


def solution(mesh):
    n, trait = mesh.shape["snp"], mesh.shape["trait"]
    return jax.shard_map(
        functools.partial(body, n, trait),
        mesh=mesh,
        in_specs=(P(None, "snp"), P("snp", "trait"), P("snp", "trait"), P(), P()),
        out_specs=P("snp", "trait"),
        check_vma=False,
    )
```
